256 devices in a mesh: row: 32 (over z, y_lo, core), col: 8 (over x, y_hi).
Axes of the slice: x: 4, y: 4 (y_hi: 2, y_lo: 2; y = y_hi * 2 + y_lo), z: 8, core: 2. Of those that a mesh axis runs over, the one named last changes fastest.
Arguments:
- activations: bfloat16 [1024, 16384], P('col', 'row'), may hold values from -6 to 6
- out_grad: bfloat16 [1024, 16384], P('col', 'row'), may hold values from -2 to 2
- gate_pre: bfloat16 [1024, 8192], P('row', 'col'), may hold values from -6 to 6
- up_pre: bfloat16 [1024, 8192], P('row', 'col'), may hold values from -6 to 6
- gate_weight: bfloat16 [16384, 8192], P('row', 'col'), may hold values from -0.046875 to 0.046875
- up_weight: bfloat16 [16384, 8192], P('row', 'col'), may hold values from -0.046875 to 0.046875
- down_weight: bfloat16 [8192, 16384], P('col', 'row'), may hold values from -0.0625 to 0.0625
Outputs:
- input_grad: bfloat16 [1024, 16384], P('col', 'row')
- gate_grad: bfloat16 [16384, 8192], P('row', 'col')
- up_grad: bfloat16 [16384, 8192], P('row', 'col')
- down_grad: bfloat16 [8192, 16384], P('col', 'row')
The draws below stay inside these ranges and needn't reach their ends.
All inputs are finite; a program needn't handle non-finite values.
Results may differ from the reference program's by a relative error of at most 0.0051.
Values may be sent and summed in bfloat16 or wider, within the bound.
A program may use at most 64 MiB of HBM per device.

```python
import jax
import jax.numpy as jnp
from jax import lax

D = 16384
PANEL = 8192
TOKENS = 1024


def raised(array, stream_key, source, target, shards_of, factor):
    owner, partner = [(jnp.arange(array.shape[dim]) // (array.shape[dim] // shards_of)).reshape([-1 if axis == dim else 1 for axis in range(array.ndim)]) for dim in (source, target)]
    chosen = jax.random.permutation(stream_key, shards_of)[partner]
    strong = (owner == chosen) | (owner == (partner + shards_of // 2) % shards_of)
    return jnp.where(strong, factor * array, array)


def block_levels(own_key, dims, cuts, smallest, largest):
    def one(position, parts):
        steps = jax.random.uniform(jax.random.fold_in(jax.random.fold_in(own_key, 6), position), (parts,), jnp.float32, smallest / len(cuts), largest / len(cuts))
        return jnp.repeat(jnp.exp(steps), dims[position] // parts).reshape((-1,) + (1,) * (len(dims) - position - 1))

    gain = one(*cuts[0])
    for cut in cuts[1:]:
        gain = gain * one(*cut)
    return gain


def noise(key, shape, width, bound, shards=(), held_as=jnp.bfloat16):
    array = jax.random.normal(key, shape, jnp.float32) * width
    if len(shards) > 0:
        array = block_levels(key, shape, shards, -0.22, 0.18) * array
    return jnp.clip(array, min=-bound, max=bound).astype(held_as)


def bell_draw_with(key, extent, width, limit, split, heavy, kind=jnp.bfloat16):
    drawn = width * jax.random.normal(key, extent, jnp.float32)
    if split:
        drawn = drawn * block_levels(key, extent, split, -0.22, 0.18)
    return jnp.clip(raised(drawn, jax.random.fold_in(key, 3), *heavy), -limit, limit).astype(kind)


def setup_inputs(seed: int = 0) -> dict:
    keys = jax.random.split(jax.random.key(seed), 8)
    activations = noise(keys[0], (TOKENS, D), 1.0, 6.0, ((0, 8), (1, 32)))
    out_grad = bell_draw_with(keys[1], (TOKENS, D), 0.25, 2.0, ((0, 8), (1, 32)), (1, 0, 32, 2.75))
    gate_pre = noise(keys[2], (TOKENS, PANEL), 1.0, 6.0, ((0, 32), (1, 8)))
    up_pre = noise(keys[3], (TOKENS, PANEL), 1.0, 6.0, ((0, 32), (1, 8)))
    gate_weight = noise(keys[4], (D, PANEL), D ** -0.5, 0.046875, ((0, 32), (1, 8)))
    up_weight = noise(keys[5], (D, PANEL), D ** -0.5, 0.046875, ((0, 32), (1, 8)))
    down_weight = noise(keys[6], (PANEL, D), PANEL ** -0.5, 0.0625, ((0, 8), (1, 32)))
    return {"activations": activations, "out_grad": out_grad, "gate_pre": gate_pre, "up_pre": up_pre, "gate_weight": gate_weight, "up_weight": up_weight, "down_weight": down_weight}


def contract_rows(left, right):
    return lax.dot_general(left, right, (((0,), (0,)), ((), ())), preferred_element_type=jnp.float32)


def contract_cols(left, right):
    return lax.dot_general(left, right, (((1,), (1,)), ((), ())), preferred_element_type=jnp.float32)


def reference(activations, out_grad, gate_pre, up_pre, gate_weight, up_weight, down_weight):
    hidden_grad = contract_cols(out_grad, down_weight)
    gate_val = gate_pre.astype(jnp.float32)
    up_val = up_pre.astype(jnp.float32)
    gate_sig = jax.nn.sigmoid(gate_val)
    swish_val = gate_val * gate_sig
    hidden = (swish_val * up_val).astype(jnp.bfloat16)
    gate_back = (hidden_grad * up_val * gate_sig * (1.0 + gate_val * (1.0 - gate_sig))).astype(jnp.bfloat16)
    up_back = (hidden_grad * swish_val).astype(jnp.bfloat16)
    down_grad = contract_rows(hidden, out_grad).astype(jnp.bfloat16)
    gate_grad = contract_rows(activations, gate_back).astype(jnp.bfloat16)
    up_grad = contract_rows(activations, up_back).astype(jnp.bfloat16)
    input_grad = (contract_cols(gate_back, gate_weight) + contract_cols(up_back, up_weight)).astype(jnp.bfloat16)
    return (input_grad, gate_grad, up_grad, down_grad)
```

```python
import jax
import jax.numpy as jnp
from jax import lax
from jax.experimental import pallas as pl
from jax.experimental.pallas import tpu as pltpu
from jax.sharding import PartitionSpec as P

MESH = pl.DeviceIdType.MESH
BF = jnp.bfloat16
F32 = jnp.float32
NZ, NX = 8, 4
CH = 2
W = 1024 // CH
N_SEM = 192


def dot_nt(left, right):
    return lax.dot_general(left, right, (((1,), (1,)), ((), ())), preferred_element_type=F32)


def dot_tn(left, right):
    return lax.dot_general(left, right, (((0,), (0,)), ((), ())), preferred_element_type=F32)


def kernel(
    acts, grad, gate, up, gw, uw, dw,
    o_in, o_gate, o_up, o_down,
    acts_all, grad_all, g_all, u_all, hg_all, gw_v, uw_v, dw_v,
    part, rc, qb, zs, zr, zls, zlr, sf, sb, ry,
    a_f, b_f, hid, gb, ub,
    far_s, far_r, near_s, near_r, own_f, ys, yr, in_v, gate_v, up_v, down_v,
    send_sem, recv_sem, loc_sem,
):
    r = lax.axis_index("row")
    c = lax.axis_index("col")
    k = lax.rem(r, 2)
    yl = lax.rem(r // 2, 2)
    z = r // 4
    yh = lax.rem(c, 2)
    x = c // 2
    zz = lambda d: lax.rem(z + d + NZ, NZ)
    xx = lambda d: lax.rem(x + d + NX, NX)
    sib = {"row": r + 1 - 2 * k}
    ylp = {"row": r + 2 - 4 * yl}
    zp = {"row": lax.rem(r + 4, 32)}
    zm = {"row": lax.rem(r + 28, 32)}
    xp = {"col": lax.rem(c + 2, 8)}
    xm = {"col": lax.rem(c + 6, 8)}
    yhp = {"col": c + 1 - 2 * yh}

    barrier = pltpu.get_barrier_semaphore()
    for peer in (sib, ylp, zp, zm, xp, xm, yhp):
        pl.semaphore_signal(barrier, inc=1, device_id=peer, device_id_type=MESH)

    n_local = [0]
    local = {}

    def fetch(name, src, dst):
        copy = pltpu.make_async_copy(src, dst, loc_sem.at[n_local[0]])
        n_local[0] += 1
        copy.start()
        local[name] = copy

    fetch("grad", grad, grad_all.at[c])
    fetch("acts", acts, acts_all.at[c])
    fetch("g", gate, g_all.at[z, yl, k])
    fetch("u", up, u_all.at[z, yl, k])
    fetch("dw", dw, dw_v)
    fetch("gw", gw, gw_v)
    fetch("uw", uw, uw_v)
    pl.semaphore_wait(barrier, 7)

    copies = {}

    def send(name, src, dst, peer):
        i = len(copies)
        copy = pltpu.make_async_remote_copy(
            src_ref=src, dst_ref=dst, send_sem=send_sem.at[i], recv_sem=recv_sem.at[i],
            device_id=peer, device_id_type=MESH,
        )
        copy.start()
        copies[name] = copy

    def got(*names):
        for name in names:
            copies[name].wait_recv()

    class Col:
        def __init__(self, name, src, dst):
            self.n, self.src, self.dst = name, src, dst

        def s0(self):
            d = self.dst.at[c]
            send(self.n + "yh", self.src, d, yhp)
            send(self.n + "p0", self.src, d, xp)
            send(self.n + "m0", self.src, d, xm)

        def s1(self):
            got(self.n + "yh")
            d = self.dst.at[2 * x + 1 - yh]
            send(self.n + "p1", d, d, xp)
            send(self.n + "m1", d, d, xm)

        def s2(self):
            got(self.n + "p0")
            d = self.dst.at[2 * xx(-1) + yh]
            send(self.n + "p2", d, d, xp)

        def s3(self):
            got(self.n + "m1")
            d = self.dst.at[2 * xx(1) + 1 - yh]
            send(self.n + "m2", d, d, xm)

        def fin(self):
            got(self.n + "p1", self.n + "m0", self.n + "p2", self.n + "m2")

    class RowY:
        def __init__(self, name, src, piece, own=None):
            self.n, self.src, self.piece, self.own = name, src, piece, own

        def both(self, d):
            return self.piece(zz(d), slice(None), k)

        def s0(self):
            n, d = self.n, self.piece(z, yl, k)
            send(n + "y", self.src, d, ylp)
            send(n + "p0", self.src, d, zp)
            send(n + "m0", self.src, d, zm)

        def s1(self):
            n, d = self.n, self.piece(z, 1 - yl, k)
            got(n + "y")
            send(n + "p0o", d, d, zp)
            send(n + "m0o", d, d, zm)
            if self.own is not None:
                local[self.own].wait()
            send(n + "s0", self.both(0), self.both(0), sib)

        def hop(self, h):
            n = self.n
            tail = ("", "o") if h == 1 else ("",)
            got(*[n + "p" + str(h - 1) + t for t in tail])
            if h < 3:
                send(n + "p" + str(h), self.both(-h), self.both(-h), zp)
            else:
                d = self.piece(zz(-h), yl, k)
                send(n + "p3", d, d, zp)
            got(*[n + "m" + str(h - 1) + t for t in tail])
            if h < 3:
                send(n + "m" + str(h), self.both(h), self.both(h), zm)
            else:
                d = self.piece(zz(h), 1 - yl, k)
                send(n + "m3", d, d, zm)
            send(n + "sp" + str(h), self.both(-h), self.both(-h), sib)
            send(n + "sm" + str(h), self.both(h), self.both(h), sib)

        def last(self):
            n = self.n
            got(n + "p3", n + "m3")
            send(n + "s4", self.both(4), self.both(4), sib)

        def fin(self):
            n = self.n
            got(*[n + t for t in ("s0", "sp1", "sm1", "sp2", "sm2", "sp3", "sm3", "s4")])

    col_g = Col("cg", grad, grad_all)
    col_a = Col("ca", acts, acts_all)
    row_g = RowY("rg", gate, lambda a, b, e: g_all.at[a, b, e], "g")
    row_u = RowY("ru", up, lambda a, b, e: u_all.at[a, b, e], "u")

    col_g.s0()
    row_g.s0()
    row_u.s0()
    col_a.s0()
    col_g.s1()
    row_g.s1()
    row_u.s1()
    col_g.s2()
    col_g.s3()
    col_a.s1()
    row_g.hop(1)
    row_u.hop(1)
    local["grad"].wait()
    local["dw"].wait()
    col_g.fin()

    for j in range(CH):

        def tile(b, carry, j=j):
            left = grad_all[pl.ds(2 * b, 2)].reshape(256, 512)
            val = dot_nt(left, dw_v[j * W : (j + 1) * W, :])
            part[j, pl.ds(2 * b, 2)] = val.reshape(2, 2, 2, 32, W)
            return carry

        lax.fori_loop(0, 4, tile, 0)
        send("core" + str(j), part.at[j, :, :, 1 - k], rc.at[j], sib)

    col_a.s2()
    col_a.s3()
    row_g.hop(2)
    row_u.hop(2)

    for j in range(CH):
        got("core" + str(j))

        def add(b, carry, j=j):
            qb[j, b] = part[j, b, :, k] + rc[j, b]
            return carry

        lax.fori_loop(0, NZ, add, 0)

    for s in range(1, 5):
        for j in range(CH):
            for way in range(2):
                first = 1 if way == j % 2 else 2
                if s < first:
                    continue
                dest = zz(5 - s) if way == 0 else zz(s - 5)
                peer = zp if way == 0 else zm
                tag = "z%d%d" % (j, way)
                val = qb[j, dest]
                if s > first:
                    got(tag + str(s - 1))
                    val = val + zr[j, way, s - 2].astype(F32)
                if s < 4:
                    zs[j, way, s - 1] = val.astype(BF)
                    send(tag + str(s), zs.at[j, way, s - 1], zr.at[j, way, s - 1], peer)
                else:
                    zls[j, way] = val
                    send(tag + str(s), zls.at[j, way], zlr.at[j, way], peer)

    row_hg = []
    for j in range(CH):
        got("z%d04" % j, "z%d14" % j)
        sf[j] = qb[j, z] + zlr[j, 0] + zlr[j, 1]
        sb[j] = sf[j, 1 - yl].astype(BF)
        send("yl%d" % j, sb.at[j], ry.at[j], ylp)
    for j in range(CH):
        got("yl%d" % j)
        hg_all[j, z, yl, k] = (sf[j, yl] + ry[j].astype(F32)).astype(BF)
        own = hg_all.at[j, z, yl, k]
        flow = RowY("rh%d" % j, own, lambda a, b, e, j=j: hg_all.at[j, a, b, e])
        flow.s0()
        row_hg.append(flow)
    row_g.hop(3)
    row_u.hop(3)
    for flow in row_hg:
        flow.s1()
    row_g.last()
    row_u.last()
    for flow in row_hg:
        flow.hop(1)
    col_a.fin()
    row_g.fin()
    row_u.fin()

    def factors(b, carry):
        g = g_all[b].reshape(128, 1024).astype(F32)
        u = u_all[b].reshape(128, 1024).astype(F32)
        s = 0.5 * (1.0 + jnp.tanh(0.5 * g))
        swish = g * s
        hid[pl.ds(pl.multiple_of(b * 128, 128), 128), :] = (swish * u).astype(BF)
        a_f[b] = u * s * (1.0 + g * (1.0 - s))
        b_f[b] = swish
        return carry

    lax.fori_loop(0, 4, factors, 0)
    for flow in row_hg:
        flow.hop(2)
    lax.fori_loop(4, 8, factors, 0)
    for flow in row_hg:
        flow.hop(3)

    def down(n, carry):
        cols = pl.ds(pl.multiple_of(n * 256, 256), 256)
        down_v[cols, :] = dot_tn(hid[:, cols], grad_all[...].reshape(1024, 512)).astype(BF)
        return carry

    lax.fori_loop(0, 2, down, 0)
    for flow in row_hg:
        flow.last()
    lax.fori_loop(2, 4, down, 0)
    out_down = pltpu.make_async_copy(down_v, o_down, loc_sem.at[8])
    out_down.start()
    for flow in row_hg:
        flow.fin()
    local["gw"].wait()
    local["uw"].wait()
    local["acts"].wait()

    def block(xb):
        for e in range(2):
            b = 2 * xb + e
            for j in range(CH):
                cols = slice(j * W, (j + 1) * W)
                hg = hg_all[j, b].reshape(128, W).astype(F32)
                gb[b, :, cols] = (hg * a_f[b, :, cols]).astype(BF)
                ub[b, :, cols] = (hg * b_f[b, :, cols]).astype(BF)
        gbv = gb[pl.ds(2 * xb, 2)].reshape(256, 1024)
        ubv = ub[pl.ds(2 * xb, 2)].reshape(256, 1024)
        return dot_nt(gbv, gw_v[...]) + dot_nt(ubv, uw_v[...])

    val = block(xx(2))
    far_s[0] = val[:, :256].astype(BF)
    far_s[1] = val[:, 256:].astype(BF)
    send("fp", far_s.at[0], far_r.at[0], xp)
    send("fm", far_s.at[1], far_r.at[1], xm)
    val = block(xx(1))
    near_s[0, :, 256:] = val[:, 256:].astype(BF)
    got("fp")
    near_s[0, :, :256] = (val[:, :256] + far_r[0].astype(F32)).astype(BF)
    send("np", near_s.at[0], near_r.at[0], xp)
    val = block(xx(-1))
    near_s[1, :, :256] = val[:, :256].astype(BF)
    got("fm")
    near_s[1, :, 256:] = (val[:, 256:] + far_r[1].astype(F32)).astype(BF)
    send("nm", near_s.at[1], near_r.at[1], xm)
    own_f[...] = block(x).reshape(2, 128, 512)

    def weight(dst, src):
        def step(n, carry):
            cols = pl.ds(pl.multiple_of(n * 256, 256), 256)
            right = src[:, :, cols].reshape(1024, 256)
            dst[:, cols] = dot_tn(acts_all[...].reshape(1024, 512), right).astype(BF)
            return carry

        lax.fori_loop(0, 4, step, 0)

    weight(gate_v, gb)
    out_gate = pltpu.make_async_copy(gate_v, o_gate, loc_sem.at[9])
    out_gate.start()
    got("np", "nm")
    own_f[...] = (
        own_f[...]
        + near_r[0].astype(F32).reshape(2, 128, 512)
        + near_r[1].astype(F32).reshape(2, 128, 512)
    )
    ys[...] = own_f[1 - yh].astype(BF)
    send("yh", ys, yr, yhp)
    weight(up_v, ub)
    out_up = pltpu.make_async_copy(up_v, o_up, loc_sem.at[10])
    out_up.start()
    got("yh")
    in_v[...] = (own_f[yh] + yr[...].astype(F32)).astype(BF)
    out_in = pltpu.make_async_copy(in_v, o_in, loc_sem.at[11])
    out_in.start()
    for copy in copies.values():
        copy.wait_send()
    for copy in (out_down, out_gate, out_up, out_in):
        copy.wait()


def per_device(activations, out_grad, gate_pre, up_pre, gate_weight, up_weight, down_weight):
    hbm = pl.BlockSpec(memory_space=pl.ANY)
    outs = pl.pallas_call(
        kernel,
        out_shape=(
            jax.ShapeDtypeStruct((128, 512), BF),
            jax.ShapeDtypeStruct((512, 1024), BF),
            jax.ShapeDtypeStruct((512, 1024), BF),
            jax.ShapeDtypeStruct((1024, 512), BF),
        ),
        in_specs=[hbm] * 7,
        out_specs=(hbm,) * 4,
        scratch_shapes=[
            pltpu.VMEM((8, 128, 512), BF),
            pltpu.VMEM((8, 128, 512), BF),
            pltpu.VMEM((8, 2, 2, 32, 1024), BF),
            pltpu.VMEM((8, 2, 2, 32, 1024), BF),
            pltpu.VMEM((CH, 8, 2, 2, 32, W), BF),
            pltpu.VMEM((512, 1024), BF),
            pltpu.VMEM((512, 1024), BF),
            pltpu.VMEM((1024, 512), BF),
            pltpu.VMEM((CH, 8, 2, 2, 32, W), F32),
            pltpu.VMEM((CH, 8, 2, 32, W), F32),
            pltpu.VMEM((CH, 8, 2, 32, W), F32),
            pltpu.VMEM((CH, 2, 3, 2, 32, W), BF),
            pltpu.VMEM((CH, 2, 3, 2, 32, W), BF),
            pltpu.VMEM((CH, 2, 2, 32, W), F32),
            pltpu.VMEM((CH, 2, 2, 32, W), F32),
            pltpu.VMEM((CH, 2, 32, W), F32),
            pltpu.VMEM((CH, 32, W), BF),
            pltpu.VMEM((CH, 32, W), BF),
            pltpu.VMEM((8, 128, 1024), F32),
            pltpu.VMEM((8, 128, 1024), F32),
            pltpu.VMEM((1024, 1024), BF),
            pltpu.VMEM((8, 128, 1024), BF),
            pltpu.VMEM((8, 128, 1024), BF),
            pltpu.VMEM((2, 256, 256), BF),
            pltpu.VMEM((2, 256, 256), BF),
            pltpu.VMEM((2, 256, 512), BF),
            pltpu.VMEM((2, 256, 512), BF),
            pltpu.VMEM((2, 128, 512), F32),
            pltpu.VMEM((128, 512), BF),
            pltpu.VMEM((128, 512), BF),
            pltpu.VMEM((128, 512), BF),
            pltpu.VMEM((512, 1024), BF),
            pltpu.VMEM((512, 1024), BF),
            pltpu.VMEM((1024, 512), BF),
            pltpu.SemaphoreType.DMA((N_SEM,)),
            pltpu.SemaphoreType.DMA((N_SEM,)),
            pltpu.SemaphoreType.DMA((12,)),
        ],
        compiler_params=pltpu.CompilerParams(
            collective_id=0, has_side_effects=True, vmem_limit_bytes=60 * 1024 * 1024
        ),
    )(activations, out_grad, gate_pre, up_pre, gate_weight, up_weight, down_weight)
    return outs


def solution(mesh):
    placed = (
        P("col", "row"),
        P("col", "row"),
        P("row", "col"),
        P("row", "col"),
        P("row", "col"),
        P("row", "col"),
        P("col", "row"),
    )
    return jax.shard_map(
        per_device,
        mesh=mesh,
        in_specs=placed,
        out_specs=(P("col", "row"), P("row", "col"), P("row", "col"), P("col", "row")),
        check_vma=False,
    )
```

```python
import jax
import jax.numpy as jnp
from jax import lax
from jax.experimental import pallas as pl
from jax.experimental.pallas import tpu as pltpu
from jax.sharding import PartitionSpec as P

MESH = pl.DeviceIdType.MESH
BF = jnp.bfloat16
F32 = jnp.float32
NZ, NX = 8, 4
CH = 2
W = 1024 // CH
N_SEM = 192


def dot_nt(left, right):
    return lax.dot_general(left, right, (((1,), (1,)), ((), ())), preferred_element_type=F32)


def dot_tn(left, right):
    return lax.dot_general(left, right, (((0,), (0,)), ((), ())), preferred_element_type=F32)


def kernel(
    acts, grad, gate, up, gw, uw, dw,
    o_in, o_gate, o_up, o_down,
    acts_all, grad_all, g_all, u_all, hg_all, gw_v, uw_v, dw_v,
    part, rc, ys_r, yr_r, zs, zr, zls, zlr,
    a_f, b_f, hid, gb, ub,
    far_s, far_r, near_s, near_r, near_f, own_f, ys, yr,
    send_sem, recv_sem, loc_sem,
):
    r = lax.axis_index("row")
    c = lax.axis_index("col")
    k = lax.rem(r, 2)
    yl = lax.rem(r // 2, 2)
    z = r // 4
    yh = lax.rem(c, 2)
    x = c // 2
    zz = lambda d: lax.rem(z + d + NZ, NZ)
    xx = lambda d: lax.rem(x + d + NX, NX)
    sib = {"row": r + 1 - 2 * k}
    ylp = {"row": r + 2 - 4 * yl}
    zp = {"row": lax.rem(r + 4, 32)}
    zm = {"row": lax.rem(r + 28, 32)}
    xp = {"col": lax.rem(c + 2, 8)}
    xm = {"col": lax.rem(c + 6, 8)}
    yhp = {"col": c + 1 - 2 * yh}

    barrier = pltpu.get_barrier_semaphore()
    for peer in (sib, ylp, zp, zm, xp, xm, yhp):
        pl.semaphore_signal(barrier, inc=1, device_id=peer, device_id_type=MESH)

    n_local = [0]
    local = {}

    def fetch(name, src, dst):
        copy = pltpu.make_async_copy(src, dst, loc_sem.at[n_local[0]])
        n_local[0] += 1
        copy.start()
        local[name] = copy

    fetch("grad", grad, grad_all.at[c])
    fetch("acts", acts, acts_all.at[c])
    fetch("g", gate, g_all.at[z, yl, k])
    fetch("u", up, u_all.at[z, yl, k])
    fetch("dw", dw, dw_v)
    fetch("gw", gw, gw_v)
    fetch("uw", uw, uw_v)
    pl.semaphore_wait(barrier, 7)

    copies = {}

    def send(name, src, dst, peer):
        i = len(copies)
        copy = pltpu.make_async_remote_copy(
            src_ref=src, dst_ref=dst, send_sem=send_sem.at[i], recv_sem=recv_sem.at[i],
            device_id=peer, device_id_type=MESH,
        )
        copy.start()
        copies[name] = copy

    def got(*names):
        for name in names:
            copies[name].wait_recv()

    rows64 = (slice(0, 64), slice(64, 128))

    class Col:
        def __init__(self, name, src, dst):
            self.n, self.src, self.dst = name, src, dst

        def s0(self):
            d = self.dst.at[c]
            send(self.n + "yh", self.src, d, yhp)
            send(self.n + "p0", self.src, d, xp)
            send(self.n + "m0", self.src, d, xm)

        def s1(self):
            got(self.n + "yh")
            d = self.dst.at[2 * x + 1 - yh]
            send(self.n + "p1", d, d, xp)
            send(self.n + "m1", d, d, xm)

        def s2(self):
            got(self.n + "p0")
            d = self.dst.at[2 * xx(-1) + yh]
            send(self.n + "p2", d, d, xp)

        def s3(self):
            got(self.n + "m1")
            d = self.dst.at[2 * xx(1) + 1 - yh]
            send(self.n + "m2", d, d, xm)

        def fin(self):
            got(self.n + "p1", self.n + "m0", self.n + "p2", self.n + "m2")

    class ColFast:
        def __init__(self, name, src, dst):
            self.n, self.src, self.dst = name, src, dst

        def s0(self):
            for h in range(2):
                send(self.n + "yh%d" % h, self.src.at[rows64[h]], self.dst.at[c, rows64[h]], yhp)
                send(self.n + "p0%d" % h, self.src.at[rows64[h]], self.dst.at[c, rows64[h]], xp)
                g = 1 - h
                send(self.n + "m0%d" % g, self.src.at[rows64[g]], self.dst.at[c, rows64[g]], xm)

        def s1(self, h):
            got(self.n + "yh%d" % h)
            d = self.dst.at[2 * x + 1 - yh, rows64[h]]
            send(self.n + "p1%d" % h, d, d, xp)
            send(self.n + "m1%d" % h, d, d, xm)

        def s2(self):
            got(self.n + "p00", self.n + "m01")
            d = self.dst.at[2 * xx(-1) + yh, rows64[0]]
            send(self.n + "p2", d, d, xp)
            d = self.dst.at[2 * xx(1) + yh, rows64[1]]
            send(self.n + "m2", d, d, xm)

        def s3(self):
            got(self.n + "p10")
            d = self.dst.at[2 * xx(-1) + 1 - yh, rows64[0]]
            send(self.n + "p3", d, d, xp)
            got(self.n + "m11")
            d = self.dst.at[2 * xx(1) + 1 - yh, rows64[1]]
            send(self.n + "m3", d, d, xm)

    class RowY:
        def __init__(self, name, src, piece, own=None):
            self.n, self.src, self.piece, self.own = name, src, piece, own

        def both(self, d):
            return self.piece(zz(d), slice(None), k)

        def s0(self):
            n, d = self.n, self.piece(z, yl, k)
            send(n + "y", self.src, d, ylp)
            send(n + "p0", self.src, d, zp)
            send(n + "m0", self.src, d, zm)

        def s1(self):
            n, d = self.n, self.piece(z, 1 - yl, k)
            got(n + "y")
            send(n + "p0o", d, d, zp)
            send(n + "m0o", d, d, zm)
            if self.own is not None:
                local[self.own].wait()
            send(n + "s0", self.both(0), self.both(0), sib)

        def hop(self, h):
            n = self.n
            tail = ("", "o") if h == 1 else ("",)
            got(*[n + "p" + str(h - 1) + t for t in tail])
            if h < 3:
                send(n + "p" + str(h), self.both(-h), self.both(-h), zp)
            else:
                d = self.piece(zz(-h), yl, k)
                send(n + "p3", d, d, zp)
            got(*[n + "m" + str(h - 1) + t for t in tail])
            if h < 3:
                send(n + "m" + str(h), self.both(h), self.both(h), zm)
            else:
                d = self.piece(zz(h), 1 - yl, k)
                send(n + "m3", d, d, zm)
            send(n + "sp" + str(h), self.both(-h), self.both(-h), sib)
            send(n + "sm" + str(h), self.both(h), self.both(h), sib)

        def last(self):
            n = self.n
            got(n + "p3", n + "m3")
            send(n + "s4", self.both(4), self.both(4), sib)

        def fin(self):
            n = self.n
            got(*[n + t for t in ("s0", "sp1", "sm1", "sp2", "sm2", "sp3", "sm3", "s4")])

    halves = [slice(j * W, (j + 1) * W) for j in range(CH)]

    class RowL:
        def __init__(self, name, ref, cols, src=None, own=None):
            self.n, self.ref, self.cols, self.src, self.own = name, ref, cols, src, own

        def pair(self, tag, d):
            at = self.ref.at[zz(d), yl, k]
            send(self.n + "y" + tag, at if self.src is None or d else self.src, at, ylp)

        def s0(self):
            for j, cols in enumerate(self.cols):
                d = self.ref.at[z, yl, k, :, cols]
                src = d if self.src is None else self.src.at[:, cols]
                send(self.n + "p0%d" % j, src, d, zp)
                send(self.n + "m0%d" % j, src, d, zm)

        def s1(self):
            self.pair("p0", 0)

        def hop(self, h):
            for way, to, sign in (("p", zp, -1), ("m", zm, 1)):
                for j, cols in enumerate(self.cols):
                    got("%s%s%d%d" % (self.n, way, h - 1, j))
                    if h < 3 or (way == "p") == (j == 0):
                        d = self.ref.at[zz(sign * h), yl, k, :, cols]
                        send("%s%s%d%d" % (self.n, way, h, j), d, d, to)
                self.pair("%s%d" % (way, h), sign * h)

        def last(self):
            for j in range(len(self.cols)):
                got(self.n + ("p30", "m31")[j])
            self.pair("p4", 4)

        def core(self, h):
            if h == 0 and self.own is not None:
                local[self.own].wait()
            for way, sign in (("p", -1), ("m", 1)):
                if way == "m" and h in (0, 4):
                    continue
                got("%sy%s%d" % (self.n, way, h))
                d = self.ref.at[zz(sign * h), :, k]
                send("%ss%s%d" % (self.n, way, h), d, d, sib)

        def fin(self):
            got(*[self.n + "sp%d" % h for h in range(5)])
            got(*[self.n + "sm%d" % h for h in range(1, 4)])

    col_g = ColFast("cg", grad, grad_all)
    col_a = Col("ca", acts, acts_all)
    row_g = RowY("rg", gate, lambda a, b, e: g_all.at[a, b, e], "g")
    row_u = RowL("ru", u_all, [slice(0, 1024)], up, "u")

    def partial(xb, tag):
        left = grad_all[pl.ds(2 * xb, 2)].reshape(256, 512)
        for j in range(CH):
            val = dot_nt(left, dw_v[j * W : (j + 1) * W, :])
            part[pl.ds(2 * xb, 2), :, :, :, halves[j]] = val.reshape(2, 2, 2, 32, W)
        send("core" + tag, part.at[pl.ds(2 * xb, 2), :, 1 - k], rc.at[pl.ds(2 * xb, 2)], sib)

    col_g.s0()
    row_g.s0()
    row_u.s0()
    col_g.s2()
    col_g.s1(0)
    col_g.s1(1)
    row_u.s1()
    row_g.s1()
    row_u.hop(1)
    local["grad"].wait()
    local["dw"].wait()
    partial(x, "0")
    row_u.core(0)
    col_g.s3()
    row_g.hop(1)
    row_u.hop(2)
    got("cgp01", "cgp11")
    partial(xx(-1), "p")
    got("cgm00", "cgm10")
    partial(xx(1), "m")
    row_u.core(1)
    row_u.hop(3)
    got("cgp2", "cgm2", "cgp3", "cgm3")
    partial(xx(2), "f")
    col_a.s0()
    got("core0", "corep", "corem", "coref")

    order = (4, 3, 5, 2, 6, 1, 7, 0)
    for d in order:
        b = zz(d)
        ys_r[d] = (part[b, 1 - yl, k] + rc[b, 1 - yl]).astype(BF)
        send("y%d" % d, ys_r.at[d], yr_r.at[d], ylp)

    def mine(d, cols):
        b = zz(d)
        return part[b, yl, k, :, cols] + rc[b, yl, :, cols] + yr_r[d, :, cols].astype(F32)

    for s in range(1, 5):
        if s == 1:
            got("y4")
        else:
            got("y%d" % (5 - s), "y%d" % (3 + s))
        for way in range(2):
            for j in range(CH):
                first = 1 if way == j else 2
                if s < first:
                    continue
                d = 5 - s if way == 0 else 3 + s
                peer = zp if way == 0 else zm
                tag = "z%d%d" % (j, way)
                val = mine(d, halves[j])
                if s > first:
                    got(tag + str(s - 1))
                    val = val + zr[j, way, s - 2].astype(F32)
                if s < 4:
                    zs[j, way, s - 1] = val.astype(BF)
                    send(tag + str(s), zs.at[j, way, s - 1], zr.at[j, way, s - 1], peer)
                else:
                    zls[j, way] = val
                    send(tag + str(s), zls.at[j, way], zlr.at[j, way], peer)
        if s == 1:
            row_g.hop(2)
            col_a.s1()
        if s == 2:
            row_u.core(2)
            row_u.last()
            col_a.s2()
            col_a.s3()
        if s == 3:
            row_g.hop(3)
            row_u.core(3)

    row_u.core(4)
    row_g.last()
    panel = RowL("rh", hg_all, halves)
    got("y0")
    for j in range(CH):
        got("z%d04" % j, "z%d14" % j)
        hg_all[z, yl, k, :, halves[j]] = (mine(0, halves[j]) + zlr[j, 0] + zlr[j, 1]).astype(BF)
    panel.s0()
    panel.s1()
    row_g.fin()
    row_u.fin()

    def factors(b, carry):
        g = g_all[b].reshape(128, 1024).astype(F32)
        u = u_all[b].reshape(128, 1024).astype(F32)
        s = 0.5 * (1.0 + jnp.tanh(0.5 * g))
        swish = g * s
        hid[pl.ds(pl.multiple_of(b * 128, 128), 128), :] = (swish * u).astype(BF)
        a_f[b] = u * s * (1.0 + g * (1.0 - s))
        b_f[b] = swish
        return carry

    lax.fori_loop(0, 4, factors, 0)
    panel.hop(1)
    panel.core(0)
    lax.fori_loop(4, 8, factors, 0)
    panel.hop(2)
    panel.core(1)

    def down(n, carry):
        cols = pl.ds(pl.multiple_of(n * 256, 256), 256)
        o_down[cols, :] = dot_tn(hid[:, cols], grad_all[...].reshape(1024, 512)).astype(BF)
        return carry

    lax.fori_loop(0, 2, down, 0)
    panel.hop(3)
    panel.core(2)
    panel.last()
    panel.core(3)
    lax.fori_loop(2, 4, down, 0)
    panel.core(4)
    col_a.fin()
    panel.fin()
    local["gw"].wait()
    local["uw"].wait()
    local["acts"].wait()

    def derive(xb):
        for e in range(2):
            b = 2 * xb + e
            hg = hg_all[b].reshape(128, 1024).astype(F32)
            gb[b] = (hg * a_f[b]).astype(BF)
            ub[b] = (hg * b_f[b]).astype(BF)

    def block(xb, side):
        gbv = gb[pl.ds(2 * xb, 2)].reshape(256, 1024)
        ubv = ub[pl.ds(2 * xb, 2)].reshape(256, 1024)
        rows = slice(256 * side, 256 * side + 256)
        return dot_nt(gbv, gw_v[rows, :]) + dot_nt(ubv, uw_v[rows, :])

    first, second = 1 - yh, yh
    derive(xx(2))
    far_s[0] = block(xx(2), 0).astype(BF).reshape(2, 128, 256)
    send("fp0", far_s.at[0, first], far_r.at[0, first], xp)
    far_s[1] = block(xx(2), 1).astype(BF).reshape(2, 128, 256)
    send("fm0", far_s.at[1, first], far_r.at[1, first], xm)
    derive(xx(1))
    near_s[0, 1] = block(xx(1), 1).astype(BF).reshape(2, 128, 256)
    send("np10", near_s.at[0, 1, first], near_r.at[0, 1, first], xp)
    send("fp1", far_s.at[0, second], far_r.at[0, second], xp)
    derive(xx(-1))
    near_s[1, 0] = block(xx(-1), 0).astype(BF).reshape(2, 128, 256)
    send("nm00", near_s.at[1, 0, first], near_r.at[1, 0, first], xm)
    send("fm1", far_s.at[1, second], far_r.at[1, second], xm)
    near_f[0] = block(xx(1), 0).reshape(2, 128, 256)
    got("fp0")
    near_s[0, 0, first] = (near_f[0, first] + far_r[0, first].astype(F32)).astype(BF)
    send("np00", near_s.at[0, 0, first], near_r.at[0, 0, first], xp)
    send("np11", near_s.at[0, 1, second], near_r.at[0, 1, second], xp)
    near_f[1] = block(xx(-1), 1).reshape(2, 128, 256)
    got("fm0")
    near_s[1, 1, first] = (near_f[1, first] + far_r[1, first].astype(F32)).astype(BF)
    send("nm10", near_s.at[1, 1, first], near_r.at[1, 1, first], xm)
    send("nm01", near_s.at[1, 0, second], near_r.at[1, 0, second], xm)
    got("fp1")
    near_s[0, 0, second] = (near_f[0, second] + far_r[0, second].astype(F32)).astype(BF)
    send("np01", near_s.at[0, 0, second], near_r.at[0, 0, second], xp)
    got("fm1")
    near_s[1, 1, second] = (near_f[1, second] + far_r[1, second].astype(F32)).astype(BF)
    send("nm11", near_s.at[1, 1, second], near_r.at[1, 1, second], xm)
    derive(x)
    for side in range(2):
        own_f[side] = block(x, side).reshape(2, 128, 256)

    def total(side, e, part_of):
        got("np%d%d" % (side, part_of), "nm%d%d" % (side, part_of))
        near = near_r[0, side, e].astype(F32) + near_r[1, side, e].astype(F32)
        return own_f[side, e] + near

    for side in range(2):
        ys[side] = total(side, first, 0).astype(BF)
        send("yh%d" % side, ys.at[side], yr.at[side], yhp)

    def weight(dst, src):
        def step(n, carry):
            cols = pl.ds(pl.multiple_of(n * 256, 256), 256)
            right = src[:, :, cols].reshape(1024, 256)
            dst[:, cols] = dot_tn(acts_all[...].reshape(1024, 512), right).astype(BF)
            return carry

        lax.fori_loop(0, 4, step, 0)

    weight(o_gate, gb)
    weight(o_up, ub)
    for side in range(2):
        val = total(side, second, 1)
        got("yh%d" % side)
        o_in[:, 256 * side : 256 * side + 256] = (val + yr[side].astype(F32)).astype(BF)
    for copy in copies.values():
        copy.wait_send()


def leave(*refs):
    sems = refs[-1]
    copies = [pltpu.make_async_copy(refs[i], refs[4 + i], sems.at[i]) for i in range(4)]
    for copy in copies:
        copy.start()
    for copy in copies:
        copy.wait()


def per_device(activations, out_grad, gate_pre, up_pre, gate_weight, up_weight, down_weight):
    hbm = pl.BlockSpec(memory_space=pl.ANY)
    outs = pl.pallas_call(
        kernel,
        out_shape=(
            pltpu.VMEM((128, 512), BF),
            pltpu.VMEM((512, 1024), BF),
            pltpu.VMEM((512, 1024), BF),
            pltpu.VMEM((1024, 512), BF),
        ),
        in_specs=[hbm] * 7,
        out_specs=(pl.BlockSpec(memory_space=pltpu.VMEM),) * 4,
        scratch_shapes=[
            pltpu.VMEM((8, 128, 512), BF),
            pltpu.VMEM((8, 128, 512), BF),
            pltpu.VMEM((8, 2, 2, 32, 1024), BF),
            pltpu.VMEM((8, 2, 2, 32, 1024), BF),
            pltpu.VMEM((8, 2, 2, 32, 1024), BF),
            pltpu.VMEM((512, 1024), BF),
            pltpu.VMEM((512, 1024), BF),
            pltpu.VMEM((1024, 512), BF),
            pltpu.VMEM((8, 2, 2, 32, 1024), F32),
            pltpu.VMEM((8, 2, 32, 1024), F32),
            pltpu.VMEM((8, 32, 1024), BF),
            pltpu.VMEM((8, 32, 1024), BF),
            pltpu.VMEM((CH, 2, 3, 32, W), BF),
            pltpu.VMEM((CH, 2, 3, 32, W), BF),
            pltpu.VMEM((CH, 2, 32, W), F32),
            pltpu.VMEM((CH, 2, 32, W), F32),
            pltpu.VMEM((8, 128, 1024), F32),
            pltpu.VMEM((8, 128, 1024), F32),
            pltpu.VMEM((1024, 1024), BF),
            pltpu.VMEM((8, 128, 1024), BF),
            pltpu.VMEM((8, 128, 1024), BF),
            pltpu.VMEM((2, 2, 128, 256), BF),
            pltpu.VMEM((2, 2, 128, 256), BF),
            pltpu.VMEM((2, 2, 2, 128, 256), BF),
            pltpu.VMEM((2, 2, 2, 128, 256), BF),
            pltpu.VMEM((2, 2, 128, 256), F32),
            pltpu.VMEM((2, 2, 128, 256), F32),
            pltpu.VMEM((2, 128, 256), BF),
            pltpu.VMEM((2, 128, 256), BF),
            pltpu.SemaphoreType.DMA((N_SEM,)),
            pltpu.SemaphoreType.DMA((N_SEM,)),
            pltpu.SemaphoreType.DMA((12,)),
        ],
        compiler_params=pltpu.CompilerParams(
            collective_id=0, has_side_effects=True, vmem_limit_bytes=56 * 1024 * 1024
        ),
    )(activations, out_grad, gate_pre, up_pre, gate_weight, up_weight, down_weight)
    return pl.pallas_call(
        leave,
        out_shape=tuple(jax.ShapeDtypeStruct(o.shape, BF) for o in outs),
        in_specs=[hbm] * 4,
        out_specs=(hbm,) * 4,
        scratch_shapes=[pltpu.SemaphoreType.DMA((4,))],
        compiler_params=pltpu.CompilerParams(vmem_limit_bytes=1024 * 1024),
    )(*outs)


def solution(mesh):
    placed = (
        P("col", "row"),
        P("col", "row"),
        P("row", "col"),
        P("row", "col"),
        P("row", "col"),
        P("row", "col"),
        P("col", "row"),
    )
    return jax.shard_map(
        per_device,
        mesh=mesh,
        in_specs=placed,
        out_specs=(P("col", "row"), P("row", "col"), P("row", "col"), P("col", "row")),
        check_vma=False,
    )
```

```python
import jax
import jax.numpy as jnp
from jax import lax
from jax.experimental import pallas as pl
from jax.experimental.pallas import tpu as pltpu
from jax.sharding import PartitionSpec as P

MESH = pl.DeviceIdType.MESH
BF = jnp.bfloat16
F32 = jnp.float32
NZ, NX = 8, 4
CH = 2
W = 1024 // CH
N_SEM = 192


def dot_nt(left, right):
    return lax.dot_general(left, right, (((1,), (1,)), ((), ())), preferred_element_type=F32)


def dot_tn(left, right):
    return lax.dot_general(left, right, (((0,), (0,)), ((), ())), preferred_element_type=F32)


def kernel(
    acts, grad, gate, up, gw, uw, dw,
    o_in, o_gate, o_up, o_down,
    acts_all, grad_all, g_all, u_all, hg_all, gw_v, uw_v, dw_v,
    part, rc, ys_r, yr_r, far_zs, far_zr, zs, zr,
    a_f, b_f, hid, gb, ub,
    far_s, far_r, near_s, near_r, near_f, own_f, ys, yr,
    send_sem, recv_sem, loc_sem,
):
    r = lax.axis_index("row")
    c = lax.axis_index("col")
    k = lax.rem(r, 2)
    yl = lax.rem(r // 2, 2)
    z = r // 4
    yh = lax.rem(c, 2)
    x = c // 2
    zz = lambda d: lax.rem(z + d + NZ, NZ)
    xx = lambda d: lax.rem(x + d + NX, NX)
    sib = {"row": r + 1 - 2 * k}
    ylp = {"row": r + 2 - 4 * yl}
    zp = {"row": lax.rem(r + 4, 32)}
    zm = {"row": lax.rem(r + 28, 32)}
    zp2 = {"row": lax.rem(r + 8, 32)}
    zm2 = {"row": lax.rem(r + 24, 32)}
    xp = {"col": lax.rem(c + 2, 8)}
    xm = {"col": lax.rem(c + 6, 8)}
    yhp = {"col": c + 1 - 2 * yh}

    barrier = pltpu.get_barrier_semaphore()
    for peer in (sib, ylp, zp, zm, zp2, zm2, xp, xm, yhp):
        pl.semaphore_signal(barrier, inc=1, device_id=peer, device_id_type=MESH)

    n_local = [0]
    local = {}

    def fetch(name, src, dst):
        copy = pltpu.make_async_copy(src, dst, loc_sem.at[n_local[0]])
        n_local[0] += 1
        copy.start()
        local[name] = copy

    fetch("grad", grad, grad_all.at[c])
    fetch("acts", acts, acts_all.at[c])
    fetch("g", gate, g_all.at[z, yl, k])
    fetch("u", up, u_all.at[z, yl, k])
    fetch("dw", dw, dw_v)
    fetch("gw", gw, gw_v)
    fetch("uw", uw, uw_v)
    pl.semaphore_wait(barrier, 9)

    copies = {}

    def send(name, src, dst, peer):
        i = len(copies)
        copy = pltpu.make_async_remote_copy(
            src_ref=src, dst_ref=dst, send_sem=send_sem.at[i], recv_sem=recv_sem.at[i],
            device_id=peer, device_id_type=MESH,
        )
        copy.start()
        copies[name] = copy

    def got(*names):
        for name in names:
            copies[name].wait_recv()

    rows64 = (slice(0, 64), slice(64, 128))

    class Col:
        def __init__(self, name, src, dst):
            self.n, self.src, self.dst = name, src, dst

        def s0(self):
            d = self.dst.at[c]
            send(self.n + "yh", self.src, d, yhp)
            send(self.n + "p0", self.src, d, xp)
            send(self.n + "m0", self.src, d, xm)

        def s1(self):
            got(self.n + "yh")
            d = self.dst.at[2 * x + 1 - yh]
            send(self.n + "p1", d, d, xp)
            send(self.n + "m1", d, d, xm)

        def s2(self):
            got(self.n + "p0")
            d = self.dst.at[2 * xx(-1) + yh]
            send(self.n + "p2", d, d, xp)

        def s3(self):
            got(self.n + "m1")
            d = self.dst.at[2 * xx(1) + 1 - yh]
            send(self.n + "m2", d, d, xm)

        def fin(self):
            got(self.n + "p1", self.n + "m0", self.n + "p2", self.n + "m2")

    class ColFast:
        def __init__(self, name, src, dst):
            self.n, self.src, self.dst = name, src, dst

        def s0(self):
            for h in range(2):
                send(self.n + "yh%d" % h, self.src.at[rows64[h]], self.dst.at[c, rows64[h]], yhp)
                send(self.n + "p0%d" % h, self.src.at[rows64[h]], self.dst.at[c, rows64[h]], xp)
                g = 1 - h
                send(self.n + "m0%d" % g, self.src.at[rows64[g]], self.dst.at[c, rows64[g]], xm)

        def s1(self, h):
            got(self.n + "yh%d" % h)
            d = self.dst.at[2 * x + 1 - yh, rows64[h]]
            send(self.n + "p1%d" % h, d, d, xp)
            send(self.n + "m1%d" % h, d, d, xm)

        def s2(self):
            got(self.n + "p00", self.n + "m01")
            d = self.dst.at[2 * xx(-1) + yh, rows64[0]]
            send(self.n + "p2", d, d, xp)
            d = self.dst.at[2 * xx(1) + yh, rows64[1]]
            send(self.n + "m2", d, d, xm)

        def s3(self):
            got(self.n + "p10")
            d = self.dst.at[2 * xx(-1) + 1 - yh, rows64[0]]
            send(self.n + "p3", d, d, xp)
            got(self.n + "m11")
            d = self.dst.at[2 * xx(1) + 1 - yh, rows64[1]]
            send(self.n + "m3", d, d, xm)

    class RowY:
        def __init__(self, name, src, piece, own=None):
            self.n, self.src, self.piece, self.own = name, src, piece, own

        def both(self, d):
            return self.piece(zz(d), slice(None), k)

        def s0(self):
            n, d = self.n, self.piece(z, yl, k)
            send(n + "y", self.src, d, ylp)
            send(n + "p0", self.src, d, zp)
            send(n + "m0", self.src, d, zm)

        def s1(self):
            n, d = self.n, self.piece(z, 1 - yl, k)
            got(n + "y")
            send(n + "p0o", d, d, zp)
            send(n + "m0o", d, d, zm)
            if self.own is not None:
                local[self.own].wait()
            send(n + "s0", self.both(0), self.both(0), sib)

        def hop(self, h):
            n = self.n
            tail = ("", "o") if h == 1 else ("",)
            got(*[n + "p" + str(h - 1) + t for t in tail])
            if h < 3:
                send(n + "p" + str(h), self.both(-h), self.both(-h), zp)
            else:
                d = self.piece(zz(-h), yl, k)
                send(n + "p3", d, d, zp)
            got(*[n + "m" + str(h - 1) + t for t in tail])
            if h < 3:
                send(n + "m" + str(h), self.both(h), self.both(h), zm)
            else:
                d = self.piece(zz(h), 1 - yl, k)
                send(n + "m3", d, d, zm)
            send(n + "sp" + str(h), self.both(-h), self.both(-h), sib)
            send(n + "sm" + str(h), self.both(h), self.both(h), sib)

        def last(self):
            n = self.n
            got(n + "p3", n + "m3")
            send(n + "s4", self.both(4), self.both(4), sib)

        def fin(self):
            n = self.n
            got(*[n + t for t in ("s0", "sp1", "sm1", "sp2", "sm2", "sp3", "sm3", "s4")])

    halves = [slice(j * W, (j + 1) * W) for j in range(CH)]

    class RowL:
        def __init__(self, name, ref, cols, src=None, own=None):
            self.n, self.ref, self.cols, self.src, self.own = name, ref, cols, src, own

        def pair(self, tag, d):
            at = self.ref.at[zz(d), yl, k]
            send(self.n + "y" + tag, at if self.src is None or d else self.src, at, ylp)

        def s0(self):
            for j, cols in enumerate(self.cols):
                d = self.ref.at[z, yl, k, :, cols]
                src = d if self.src is None else self.src.at[:, cols]
                send(self.n + "p0%d" % j, src, d, zp)
                send(self.n + "m0%d" % j, src, d, zm)

        def s1(self):
            self.pair("p0", 0)

        def hop_z(self, h):
            for way, to, sign in (("p", zp, -1), ("m", zm, 1)):
                for j, cols in enumerate(self.cols):
                    got("%s%s%d%d" % (self.n, way, h - 1, j))
                    if h < 3 or (way == "p") == (j == 0):
                        d = self.ref.at[zz(sign * h), yl, k, :, cols]
                        send("%s%s%d%d" % (self.n, way, h, j), d, d, to)

        def pairs(self, h):
            for way, sign in (("p", -1), ("m", 1)):
                self.pair("%s%d" % (way, h), sign * h)

        def last(self):
            for j in range(len(self.cols)):
                got(self.n + ("p30", "m31")[j])
            self.pair("p4", 4)

        def core(self, h):
            if h == 0 and self.own is not None:
                local[self.own].wait()
            for way, sign in (("p", -1), ("m", 1)):
                if way == "m" and h in (0, 4):
                    continue
                got("%sy%s%d" % (self.n, way, h))
                d = self.ref.at[zz(sign * h), :, k]
                send("%ss%s%d" % (self.n, way, h), d, d, sib)

        def fin(self):
            got(*[self.n + "sp%d" % h for h in range(5)])
            got(*[self.n + "sm%d" % h for h in range(1, 4)])

    class Panel:
        def at(self, d, j):
            return hg_all.at[zz(d), yl, k, :, halves[j]]

        def s0(self):
            for j in range(CH):
                for name, to in (("2p", zp2), ("2m", zm2), ("1p", zp), ("1m", zm)):
                    send("h%s%d" % (name, j), self.at(0, j), self.at(0, j), to)
            for j in range(CH):
                self.pair(0, j)

        def pair(self, d, j):
            send("hy%d%d" % (d, j), self.at(d, j), self.at(d, j), ylp)

        def relay(self, j):
            for way, d, to, on in (("p", -2, zp, zp2), ("m", 2, zm, zm2)):
                got("h2%s%d" % (way, j))
                at = self.at(d, j)
                send("h3%s%d" % (way, j), at, at, to)
                if (way == "p") == (j == 0):
                    send("h4%s%d" % (way, j), at, at, on)
                self.pair(d, j)

        def take(self, name, j, d):
            got("h%s%d" % (name, j))
            self.pair(d, j)

        def core(self, *ds):
            for d in ds:
                got("hy%d0" % d, "hy%d1" % d)
                at = hg_all.at[zz(d), :, k]
                send("hs%d" % d, at, at, sib)

        def fin(self):
            got(*["hs%d" % d for d in (0, -1, 1, -2, 2, -3, 3, 4)])

    col_g = ColFast("cg", grad, grad_all)
    col_a = Col("ca", acts, acts_all)
    row_g = RowY("rg", gate, lambda a, b, e: g_all.at[a, b, e], "g")
    row_u = RowL("ru", u_all, [slice(0, 1024)], up, "u")

    def partial(xb, tag):
        left = grad_all[pl.ds(2 * xb, 2)].reshape(256, 512)
        for j in range(CH):
            val = dot_nt(left, dw_v[j * W : (j + 1) * W, :])
            part[pl.ds(2 * xb, 2), :, :, :, halves[j]] = val.reshape(2, 2, 2, 32, W)
        send("core" + tag, part.at[pl.ds(2 * xb, 2), :, 1 - k], rc.at[pl.ds(2 * xb, 2)], sib)

    col_g.s0()
    row_u.s0()
    row_g.s0()
    col_g.s2()
    col_g.s1(0)
    col_g.s1(1)
    row_u.s1()
    row_g.s1()
    row_u.hop_z(1)
    row_u.pairs(1)
    local["grad"].wait()
    local["dw"].wait()
    partial(x, "0")
    col_g.s3()
    got("cgp01", "cgp11")
    partial(xx(-1), "p")
    got("cgm00", "cgm10")
    partial(xx(1), "m")
    row_u.hop_z(2)
    row_u.pairs(2)
    row_g.hop(1)
    got("cgp2", "cgm2", "cgp3", "cgm3")
    partial(xx(2), "f")
    got("core0", "corep", "corem", "coref")

    def give(d, j):
        b, cols = zz(d), halves[j]
        ys_r[d, :, cols] = (part[b, 1 - yl, k, :, cols] + rc[b, 1 - yl, :, cols]).astype(BF)
        send("y%d%d" % (d, j), ys_r.at[d, :, cols], yr_r.at[d, :, cols], ylp)

    for d, j in ((4, 0), (4, 1), (3, 0), (5, 0), (3, 1), (5, 1), (2, 0), (6, 0), (2, 1), (6, 1)):
        give(d, j)
    for d in (1, 7, 0):
        give(d, 0)
        give(d, 1)

    def mine(d, j):
        b, cols = zz(d), halves[j]
        got("y%d%d" % (d, j))
        return part[b, yl, k, :, cols] + rc[b, yl, :, cols] + yr_r[d, :, cols].astype(F32)

    def hand(stage, way, j, val, peer):
        zs[stage, way, :, halves[j]] = val.astype(BF)
        at = (stage, way, slice(None), halves[j])
        send("z%d%d%d" % (stage, way, j), zs.at[at], zr.at[at], peer)

    for way, peer in enumerate((zp2, zm2)):
        far_zs[way] = mine(4, way).astype(BF)
        send("z4%d" % way, far_zs.at[way], far_zr.at[way], peer)
    for j in range(CH):
        for way, d, peer in ((0, 3, zp), (1, 5, zm)):
            hand(0, way, j, mine(d, j), peer)
    col_a.s0()
    row_u.core(0)
    row_u.core(1)
    for j in range(CH):
        for way, d, peer in ((0, 2, zp2), (1, 6, zm2)):
            val = mine(d, j)
            got("z0%d%d" % (way, j))
            val = val + zr[0, way, :, halves[j]].astype(F32)
            if way == j:
                got("z4%d" % way)
                val = val + far_zr[way].astype(F32)
            hand(1, way, j, val, peer)
    for j in range(CH):
        for way, d, peer in ((0, 1, zp), (1, 7, zm)):
            hand(2, way, j, mine(d, j), peer)
    row_u.hop_z(3)
    row_u.pairs(3)
    row_g.hop(2)
    col_a.s1()
    row_u.core(2)
    for j in range(CH):
        val = mine(0, j)
        for stage in (2, 1):
            for way in range(2):
                got("z%d%d%d" % (stage, way, j))
                val = val + zr[stage, way, :, halves[j]].astype(F32)
        hg_all[z, yl, k, :, halves[j]] = val.astype(BF)
    panel = Panel()
    panel.s0()
    row_u.last()
    row_g.hop(3)
    row_u.core(3)
    col_a.s2()
    col_a.s3()

    def factors(b, carry):
        g = g_all[b].reshape(128, 1024).astype(F32)
        u = u_all[b].reshape(128, 1024).astype(F32)
        s = 0.5 * (1.0 + jnp.tanh(0.5 * g))
        swish = g * s
        hid[pl.ds(pl.multiple_of(b * 128, 128), 128), :] = (swish * u).astype(BF)
        a_f[b] = u * s * (1.0 + g * (1.0 - s))
        b_f[b] = swish
        return carry

    panel.relay(0)
    panel.relay(1)
    for j in range(CH):
        panel.take("1p", j, -1)
        panel.take("1m", j, 1)
    row_u.core(4)
    row_g.last()
    panel.core(0)
    row_u.fin()
    row_g.fin()
    lax.fori_loop(0, 3, factors, 0)

    def down(n, carry):
        cols = pl.ds(pl.multiple_of(n * 256, 256), 256)
        o_down[cols, :] = dot_tn(hid[:, cols], grad_all[...].reshape(1024, 512)).astype(BF)
        return carry

    panel.take("4p", 0, 4)
    for j in range(CH):
        panel.take("3p", j, -3)
        panel.take("3m", j, 3)
    panel.take("4m", 1, 4)
    panel.core(-2, 2)
    lax.fori_loop(3, 8, factors, 0)
    panel.core(-1, 1)
    lax.fori_loop(0, 4, down, 0)
    panel.core(-3, 3, 4)
    col_a.fin()
    panel.fin()
    local["gw"].wait()
    local["uw"].wait()
    local["acts"].wait()

    def derive(xb):
        for e in range(2):
            b = 2 * xb + e
            hg = hg_all[b].reshape(128, 1024).astype(F32)
            gb[b] = (hg * a_f[b]).astype(BF)
            ub[b] = (hg * b_f[b]).astype(BF)

    def block(xb, side):
        gbv = gb[pl.ds(2 * xb, 2)].reshape(256, 1024)
        ubv = ub[pl.ds(2 * xb, 2)].reshape(256, 1024)
        rows = slice(256 * side, 256 * side + 256)
        return dot_nt(gbv, gw_v[rows, :]) + dot_nt(ubv, uw_v[rows, :])

    first, second = 1 - yh, yh
    derive(xx(2))
    far_s[0] = block(xx(2), 0).astype(BF).reshape(2, 128, 256)
    send("fp0", far_s.at[0, first], far_r.at[0, first], xp)
    far_s[1] = block(xx(2), 1).astype(BF).reshape(2, 128, 256)
    send("fm0", far_s.at[1, first], far_r.at[1, first], xm)
    derive(xx(1))
    near_s[0, 1] = block(xx(1), 1).astype(BF).reshape(2, 128, 256)
    send("np10", near_s.at[0, 1, first], near_r.at[0, 1, first], xp)
    send("fp1", far_s.at[0, second], far_r.at[0, second], xp)
    derive(xx(-1))
    near_s[1, 0] = block(xx(-1), 0).astype(BF).reshape(2, 128, 256)
    send("nm00", near_s.at[1, 0, first], near_r.at[1, 0, first], xm)
    send("fm1", far_s.at[1, second], far_r.at[1, second], xm)
    near_f[0] = block(xx(1), 0).reshape(2, 128, 256)
    got("fp0")
    near_s[0, 0, first] = (near_f[0, first] + far_r[0, first].astype(F32)).astype(BF)
    send("np00", near_s.at[0, 0, first], near_r.at[0, 0, first], xp)
    send("np11", near_s.at[0, 1, second], near_r.at[0, 1, second], xp)
    near_f[1] = block(xx(-1), 1).reshape(2, 128, 256)
    got("fm0")
    near_s[1, 1, first] = (near_f[1, first] + far_r[1, first].astype(F32)).astype(BF)
    send("nm10", near_s.at[1, 1, first], near_r.at[1, 1, first], xm)
    send("nm01", near_s.at[1, 0, second], near_r.at[1, 0, second], xm)
    got("fp1")
    near_s[0, 0, second] = (near_f[0, second] + far_r[0, second].astype(F32)).astype(BF)
    send("np01", near_s.at[0, 0, second], near_r.at[0, 0, second], xp)
    got("fm1")
    near_s[1, 1, second] = (near_f[1, second] + far_r[1, second].astype(F32)).astype(BF)
    send("nm11", near_s.at[1, 1, second], near_r.at[1, 1, second], xm)
    derive(x)
    for side in range(2):
        own_f[side] = block(x, side).reshape(2, 128, 256)

    def total(side, e, part_of):
        got("np%d%d" % (side, part_of), "nm%d%d" % (side, part_of))
        near = near_r[0, side, e].astype(F32) + near_r[1, side, e].astype(F32)
        return own_f[side, e] + near

    for side in range(2):
        ys[side] = total(side, first, 0).astype(BF)
        send("yh%d" % side, ys.at[side], yr.at[side], yhp)

    def weight(dst, src):
        def step(n, carry):
            cols = pl.ds(pl.multiple_of(n * 256, 256), 256)
            right = src[:, :, cols].reshape(1024, 256)
            dst[:, cols] = dot_tn(acts_all[...].reshape(1024, 512), right).astype(BF)
            return carry

        lax.fori_loop(0, 4, step, 0)

    weight(o_gate, gb)
    weight(o_up, ub)
    for side in range(2):
        val = total(side, second, 1)
        got("yh%d" % side)
        o_in[:, 256 * side : 256 * side + 256] = (val + yr[side].astype(F32)).astype(BF)
    for copy in copies.values():
        copy.wait_send()


def leave(*refs):
    sems = refs[-1]
    copies = [pltpu.make_async_copy(refs[i], refs[4 + i], sems.at[i]) for i in range(4)]
    for copy in copies:
        copy.start()
    for copy in copies:
        copy.wait()


def per_device(activations, out_grad, gate_pre, up_pre, gate_weight, up_weight, down_weight):
    hbm = pl.BlockSpec(memory_space=pl.ANY)
    outs = pl.pallas_call(
        kernel,
        out_shape=(
            pltpu.VMEM((128, 512), BF),
            pltpu.VMEM((512, 1024), BF),
            pltpu.VMEM((512, 1024), BF),
            pltpu.VMEM((1024, 512), BF),
        ),
        in_specs=[hbm] * 7,
        out_specs=(pl.BlockSpec(memory_space=pltpu.VMEM),) * 4,
        scratch_shapes=[
            pltpu.VMEM((8, 128, 512), BF),
            pltpu.VMEM((8, 128, 512), BF),
            pltpu.VMEM((8, 2, 2, 32, 1024), BF),
            pltpu.VMEM((8, 2, 2, 32, 1024), BF),
            pltpu.VMEM((8, 2, 2, 32, 1024), BF),
            pltpu.VMEM((512, 1024), BF),
            pltpu.VMEM((512, 1024), BF),
            pltpu.VMEM((1024, 512), BF),
            pltpu.VMEM((8, 2, 2, 32, 1024), F32),
            pltpu.VMEM((8, 2, 32, 1024), F32),
            pltpu.VMEM((8, 32, 1024), BF),
            pltpu.VMEM((8, 32, 1024), BF),
            pltpu.VMEM((2, 32, W), BF),
            pltpu.VMEM((2, 32, W), BF),
            pltpu.VMEM((3, 2, 32, 1024), BF),
            pltpu.VMEM((3, 2, 32, 1024), BF),
            pltpu.VMEM((8, 128, 1024), F32),
            pltpu.VMEM((8, 128, 1024), F32),
            pltpu.VMEM((1024, 1024), BF),
            pltpu.VMEM((8, 128, 1024), BF),
            pltpu.VMEM((8, 128, 1024), BF),
            pltpu.VMEM((2, 2, 128, 256), BF),
            pltpu.VMEM((2, 2, 128, 256), BF),
            pltpu.VMEM((2, 2, 2, 128, 256), BF),
            pltpu.VMEM((2, 2, 2, 128, 256), BF),
            pltpu.VMEM((2, 2, 128, 256), F32),
            pltpu.VMEM((2, 2, 128, 256), F32),
            pltpu.VMEM((2, 128, 256), BF),
            pltpu.VMEM((2, 128, 256), BF),
            pltpu.SemaphoreType.DMA((N_SEM,)),
            pltpu.SemaphoreType.DMA((N_SEM,)),
            pltpu.SemaphoreType.DMA((12,)),
        ],
        compiler_params=pltpu.CompilerParams(
            collective_id=0, has_side_effects=True, vmem_limit_bytes=56 * 1024 * 1024
        ),
    )(activations, out_grad, gate_pre, up_pre, gate_weight, up_weight, down_weight)
    return pl.pallas_call(
        leave,
        out_shape=tuple(jax.ShapeDtypeStruct(o.shape, BF) for o in outs),
        in_specs=[hbm] * 4,
        out_specs=(hbm,) * 4,
        scratch_shapes=[pltpu.SemaphoreType.DMA((4,))],
        compiler_params=pltpu.CompilerParams(vmem_limit_bytes=1024 * 1024),
    )(*outs)


def solution(mesh):
    placed = (
        P("col", "row"),
        P("col", "row"),
        P("row", "col"),
        P("row", "col"),
        P("row", "col"),
        P("row", "col"),
        P("col", "row"),
    )
    return jax.shard_map(
        per_device,
        mesh=mesh,
        in_specs=placed,
        out_specs=(P("col", "row"), P("row", "col"), P("row", "col"), P("col", "row")),
        check_vma=False,
    )
```

```python
import math

import jax
import jax.numpy as jnp
from jax import lax
from jax.experimental import pallas as pl
from jax.experimental.pallas import tpu as pltpu
from jax.sharding import PartitionSpec as P

MESH = pl.DeviceIdType.MESH
BF = jnp.bfloat16
F32 = jnp.float32
NZ, NX = 8, 4
CH = 2
W = 1024 // CH
N_RECV = 149
N_SEND = 6
UNIT = 32 * 1024


def dot_nt(left, right):
    return lax.dot_general(left, right, (((1,), (1,)), ((), ())), preferred_element_type=F32)


def dot_tn(left, right):
    return lax.dot_general(left, right, (((0,), (0,)), ((), ())), preferred_element_type=F32)


def kernel(
    acts, grad, gate, up, gw, uw, dw,
    o_in, o_gate, o_up, o_down,
    acts_all, grad_all, g_all, u_all, hg_all, gw_v, uw_v, dw_v,
    part, rc, ys_r, yr_r, far_zs, far_zr, zs, zr,
    a_f, b_f, hid, gb, ub,
    far_s, far_r, near_s, near_r, near_f, own_f, ys, yr,
    send_sem, recv_sem, loc_sem,
):
    r = lax.axis_index("row")
    c = lax.axis_index("col")
    k = lax.rem(r, 2)
    yl = lax.rem(r // 2, 2)
    z = r // 4
    yh = lax.rem(c, 2)
    x = c // 2
    zz = lambda d: lax.rem(z + d + NZ, NZ)
    xx = lambda d: lax.rem(x + d + NX, NX)
    sib = {"row": r + 1 - 2 * k}
    ylp = {"row": r + 2 - 4 * yl}
    zp = {"row": lax.rem(r + 4, 32)}
    zm = {"row": lax.rem(r + 28, 32)}
    zp2 = {"row": lax.rem(r + 8, 32)}
    zm2 = {"row": lax.rem(r + 24, 32)}
    xp = {"col": lax.rem(c + 2, 8)}
    xm = {"col": lax.rem(c + 6, 8)}
    yhp = {"col": c + 1 - 2 * yh}

    barrier = pltpu.get_barrier_semaphore()
    for peer in (sib, ylp, zp, zm, zp2, zm2, xp, xm, yhp):
        pl.semaphore_signal(barrier, inc=1, device_id=peer, device_id_type=MESH)

    n_local = [0]
    local = {}

    def fetch(name, src, dst):
        copy = pltpu.make_async_copy(src, dst, loc_sem.at[n_local[0]])
        n_local[0] += 1
        copy.start()
        local[name] = copy

    fetch("grad", grad, grad_all.at[c])
    fetch("acts", acts, acts_all.at[c])
    fetch("g", gate, g_all.at[z, yl, k])
    fetch("u", up, u_all.at[z, yl, k])
    fetch("dw", dw, dw_v)
    fetch("gw", gw, gw_v)
    fetch("uw", uw, uw_v)
    pl.semaphore_wait(barrier, 9)

    copies = {}
    sent = [0]

    def send(name, src, dst, peer):
        i = len(copies)
        units = math.prod(src.shape) * src.dtype.itemsize // UNIT
        if sent[-1] + units > 64:
            sent.append(0)
        sent[-1] += units
        copy = pltpu.make_async_remote_copy(
            src_ref=src, dst_ref=dst, send_sem=send_sem.at[len(sent) - 1], recv_sem=recv_sem.at[i],
            device_id=peer, device_id_type=MESH,
        )
        copy.start()
        copies[name] = copy

    def got(*names):
        for name in names:
            copies[name].wait_recv()

    rows64 = (slice(0, 64), slice(64, 128))

    class Col:
        def __init__(self, name, src, dst):
            self.n, self.src, self.dst = name, src, dst

        def s0(self):
            d = self.dst.at[c]
            send(self.n + "yh", self.src, d, yhp)
            send(self.n + "p0", self.src, d, xp)
            send(self.n + "m0", self.src, d, xm)

        def s1(self):
            got(self.n + "yh")
            d = self.dst.at[2 * x + 1 - yh]
            send(self.n + "p1", d, d, xp)
            send(self.n + "m1", d, d, xm)

        def s2(self):
            got(self.n + "p0")
            d = self.dst.at[2 * xx(-1) + yh]
            send(self.n + "p2", d, d, xp)

        def s3(self):
            got(self.n + "m1")
            d = self.dst.at[2 * xx(1) + 1 - yh]
            send(self.n + "m2", d, d, xm)

        def fin(self):
            got(self.n + "p1", self.n + "m0", self.n + "p2", self.n + "m2")

    class ColFast:
        def __init__(self, name, src, dst):
            self.n, self.src, self.dst = name, src, dst

        def s0(self):
            for h in range(2):
                send(self.n + "yh%d" % h, self.src.at[rows64[h]], self.dst.at[c, rows64[h]], yhp)
                send(self.n + "p0%d" % h, self.src.at[rows64[h]], self.dst.at[c, rows64[h]], xp)
                g = 1 - h
                send(self.n + "m0%d" % g, self.src.at[rows64[g]], self.dst.at[c, rows64[g]], xm)

        def s1(self, h):
            got(self.n + "yh%d" % h)
            d = self.dst.at[2 * x + 1 - yh, rows64[h]]
            send(self.n + "p1%d" % h, d, d, xp)
            send(self.n + "m1%d" % h, d, d, xm)

        def s2(self):
            got(self.n + "p00", self.n + "m01")
            d = self.dst.at[2 * xx(-1) + yh, rows64[0]]
            send(self.n + "p2", d, d, xp)
            d = self.dst.at[2 * xx(1) + yh, rows64[1]]
            send(self.n + "m2", d, d, xm)

        def s3(self):
            got(self.n + "p10")
            d = self.dst.at[2 * xx(-1) + 1 - yh, rows64[0]]
            send(self.n + "p3", d, d, xp)
            got(self.n + "m11")
            d = self.dst.at[2 * xx(1) + 1 - yh, rows64[1]]
            send(self.n + "m3", d, d, xm)

    class RowY:
        def __init__(self, name, src, piece, own=None):
            self.n, self.src, self.piece, self.own = name, src, piece, own

        def both(self, d):
            return self.piece(zz(d), slice(None), k)

        def s0(self):
            n, d = self.n, self.piece(z, yl, k)
            send(n + "y", self.src, d, ylp)
            send(n + "p0", self.src, d, zp)
            send(n + "m0", self.src, d, zm)

        def s1(self):
            n, d = self.n, self.piece(z, 1 - yl, k)
            got(n + "y")
            send(n + "p0o", d, d, zp)
            send(n + "m0o", d, d, zm)
            if self.own is not None:
                local[self.own].wait()
            send(n + "s0", self.both(0), self.both(0), sib)

        def hop(self, h):
            n = self.n
            tail = ("", "o") if h == 1 else ("",)
            got(*[n + "p" + str(h - 1) + t for t in tail])
            if h < 3:
                send(n + "p" + str(h), self.both(-h), self.both(-h), zp)
            else:
                d = self.piece(zz(-h), yl, k)
                send(n + "p3", d, d, zp)
            got(*[n + "m" + str(h - 1) + t for t in tail])
            if h < 3:
                send(n + "m" + str(h), self.both(h), self.both(h), zm)
            else:
                d = self.piece(zz(h), 1 - yl, k)
                send(n + "m3", d, d, zm)
            send(n + "sp" + str(h), self.both(-h), self.both(-h), sib)
            send(n + "sm" + str(h), self.both(h), self.both(h), sib)

        def last(self):
            n = self.n
            got(n + "p3", n + "m3")
            send(n + "s4", self.both(4), self.both(4), sib)

        def fin(self):
            n = self.n
            got(*[n + t for t in ("s0", "sp1", "sm1", "sp2", "sm2", "sp3", "sm3", "s4")])

    halves = [slice(j * W, (j + 1) * W) for j in range(CH)]

    class RowL:
        def __init__(self, name, ref, cols, src=None, own=None):
            self.n, self.ref, self.cols, self.src, self.own = name, ref, cols, src, own

        def pair(self, tag, d):
            at = self.ref.at[zz(d), yl, k]
            send(self.n + "y" + tag, at if self.src is None or d else self.src, at, ylp)

        def s0(self):
            for j, cols in enumerate(self.cols):
                d = self.ref.at[z, yl, k, :, cols]
                src = d if self.src is None else self.src.at[:, cols]
                send(self.n + "p0%d" % j, src, d, zp)
                send(self.n + "m0%d" % j, src, d, zm)

        def s1(self):
            self.pair("p0", 0)

        def hop_z(self, h):
            for way, to, sign in (("p", zp, -1), ("m", zm, 1)):
                for j, cols in enumerate(self.cols):
                    got("%s%s%d%d" % (self.n, way, h - 1, j))
                    if h < 3 or (way == "p") == (j == 0):
                        d = self.ref.at[zz(sign * h), yl, k, :, cols]
                        send("%s%s%d%d" % (self.n, way, h, j), d, d, to)

        def pairs(self, h):
            for way, sign in (("p", -1), ("m", 1)):
                self.pair("%s%d" % (way, h), sign * h)

        def last(self):
            for j in range(len(self.cols)):
                got(self.n + ("p30", "m31")[j])
            self.pair("p4", 4)

        def core(self, h):
            if h == 0 and self.own is not None:
                local[self.own].wait()
            for way, sign in (("p", -1), ("m", 1)):
                if way == "m" and h in (0, 4):
                    continue
                got("%sy%s%d" % (self.n, way, h))
                d = self.ref.at[zz(sign * h), :, k]
                send("%ss%s%d" % (self.n, way, h), d, d, sib)

        def fin(self):
            got(*[self.n + "sp%d" % h for h in range(5)])
            got(*[self.n + "sm%d" % h for h in range(1, 4)])

    class Panel:
        def at(self, d, j):
            return hg_all.at[zz(d), yl, k, :, halves[j]]

        def s0(self):
            for j in range(CH):
                for name, to in (("2p", zp2), ("2m", zm2), ("1p", zp), ("1m", zm)):
                    send("h%s%d" % (name, j), self.at(0, j), self.at(0, j), to)
            for j in range(CH):
                self.pair(0, j)

        def pair(self, d, j):
            send("hy%d%d" % (d, j), self.at(d, j), self.at(d, j), ylp)

        def relay(self, j):
            for way, d, to, on in (("p", -2, zp, zp2), ("m", 2, zm, zm2)):
                got("h2%s%d" % (way, j))
                at = self.at(d, j)
                send("h3%s%d" % (way, j), at, at, to)
                if (way == "p") == (j == 0):
                    send("h4%s%d" % (way, j), at, at, on)
                self.pair(d, j)

        def take(self, name, j, d):
            got("h%s%d" % (name, j))
            self.pair(d, j)

        def core(self, *ds):
            for d in ds:
                got("hy%d0" % d, "hy%d1" % d)
                at = hg_all.at[zz(d), :, k]
                send("hs%d" % d, at, at, sib)

        def fin(self):
            got(*["hs%d" % d for d in (0, -1, 1, -2, 2, -3, 3, 4)])

    col_g = ColFast("cg", grad, grad_all)
    col_a = Col("ca", acts, acts_all)
    row_g = RowY("rg", gate, lambda a, b, e: g_all.at[a, b, e], "g")
    row_u = RowL("ru", u_all, [slice(0, 1024)], up, "u")

    def partial(xb, tag):
        left = grad_all[pl.ds(2 * xb, 2)].reshape(256, 512)
        for j in range(CH):
            val = dot_nt(left, dw_v[j * W : (j + 1) * W, :])
            part[pl.ds(2 * xb, 2), :, :, :, halves[j]] = val.reshape(2, 2, 2, 32, W)
        send("core" + tag, part.at[pl.ds(2 * xb, 2), :, 1 - k], rc.at[pl.ds(2 * xb, 2)], sib)

    col_g.s0()
    row_u.s0()
    row_g.s0()
    col_g.s2()
    col_g.s1(0)
    col_g.s1(1)
    row_u.s1()
    row_g.s1()
    row_u.hop_z(1)
    row_u.pairs(1)
    local["grad"].wait()
    local["dw"].wait()
    partial(x, "0")
    col_g.s3()
    got("cgp01", "cgp11")
    partial(xx(-1), "p")
    got("cgm00", "cgm10")
    partial(xx(1), "m")
    row_u.hop_z(2)
    row_u.pairs(2)
    row_g.hop(1)
    got("cgp2", "cgm2", "cgp3", "cgm3")
    partial(xx(2), "f")
    got("core0", "corep", "corem", "coref")

    def give(d, j):
        b, cols = zz(d), halves[j]
        ys_r[d, :, cols] = (part[b, 1 - yl, k, :, cols] + rc[b, 1 - yl, :, cols]).astype(BF)
        send("y%d%d" % (d, j), ys_r.at[d, :, cols], yr_r.at[d, :, cols], ylp)

    for d, j in ((4, 0), (4, 1), (3, 0), (5, 0), (3, 1), (5, 1), (2, 0), (6, 0), (2, 1), (6, 1)):
        give(d, j)
    for d in (1, 7, 0):
        give(d, 0)
        give(d, 1)

    def mine(d, j):
        b, cols = zz(d), halves[j]
        got("y%d%d" % (d, j))
        return part[b, yl, k, :, cols] + rc[b, yl, :, cols] + yr_r[d, :, cols].astype(F32)

    def hand(stage, way, j, val, peer):
        zs[stage, way, :, halves[j]] = val.astype(BF)
        at = (stage, way, slice(None), halves[j])
        send("z%d%d%d" % (stage, way, j), zs.at[at], zr.at[at], peer)

    for way, peer in enumerate((zp2, zm2)):
        far_zs[way] = mine(4, way).astype(BF)
        send("z4%d" % way, far_zs.at[way], far_zr.at[way], peer)
    for j in range(CH):
        for way, d, peer in ((0, 3, zp), (1, 5, zm)):
            hand(0, way, j, mine(d, j), peer)
    col_a.s0()
    row_u.core(0)
    row_u.core(1)
    for j in range(CH):
        for way, d, peer in ((0, 2, zp2), (1, 6, zm2)):
            val = mine(d, j)
            got("z0%d%d" % (way, j))
            val = val + zr[0, way, :, halves[j]].astype(F32)
            if way == j:
                got("z4%d" % way)
                val = val + far_zr[way].astype(F32)
            hand(1, way, j, val, peer)
    for j in range(CH):
        for way, d, peer in ((0, 1, zp), (1, 7, zm)):
            hand(2, way, j, mine(d, j), peer)
    row_u.hop_z(3)
    row_u.pairs(3)
    row_g.hop(2)
    col_a.s1()
    row_u.core(2)
    for j in range(CH):
        val = mine(0, j)
        for stage in (2, 1):
            for way in range(2):
                got("z%d%d%d" % (stage, way, j))
                val = val + zr[stage, way, :, halves[j]].astype(F32)
        hg_all[z, yl, k, :, halves[j]] = val.astype(BF)
    panel = Panel()
    panel.s0()
    row_u.last()
    row_g.hop(3)
    row_u.core(3)
    col_a.s2()
    col_a.s3()

    def factors(b, carry):
        g = g_all[b].reshape(128, 1024).astype(F32)
        u = u_all[b].reshape(128, 1024).astype(F32)
        s = 0.5 * (1.0 + jnp.tanh(0.5 * g))
        swish = g * s
        hid[pl.ds(pl.multiple_of(b * 128, 128), 128), :] = (swish * u).astype(BF)
        a_f[b] = u * s * (1.0 + g * (1.0 - s))
        b_f[b] = swish
        return carry

    panel.relay(0)
    panel.relay(1)
    for j in range(CH):
        panel.take("1p", j, -1)
        panel.take("1m", j, 1)
    row_u.core(4)
    row_g.last()
    panel.core(0)
    row_u.fin()
    row_g.fin()
    lax.fori_loop(0, 3, factors, 0)

    def down(n, carry):
        cols = pl.ds(pl.multiple_of(n * 256, 256), 256)
        o_down[cols, :] = dot_tn(hid[:, cols], grad_all[...].reshape(1024, 512)).astype(BF)
        return carry

    panel.take("4p", 0, 4)
    for j in range(CH):
        panel.take("3p", j, -3)
        panel.take("3m", j, 3)
    panel.take("4m", 1, 4)
    panel.core(-2, 2)
    lax.fori_loop(3, 8, factors, 0)
    panel.core(-1, 1)
    lax.fori_loop(0, 4, down, 0)
    panel.core(-3, 3, 4)
    col_a.fin()
    panel.fin()
    local["gw"].wait()
    local["uw"].wait()
    local["acts"].wait()

    def derive(xb):
        for e in range(2):
            b = 2 * xb + e
            hg = hg_all[b].reshape(128, 1024).astype(F32)
            gb[b] = (hg * a_f[b]).astype(BF)
            ub[b] = (hg * b_f[b]).astype(BF)

    def block(xb, side):
        gbv = gb[pl.ds(2 * xb, 2)].reshape(256, 1024)
        ubv = ub[pl.ds(2 * xb, 2)].reshape(256, 1024)
        rows = slice(256 * side, 256 * side + 256)
        return dot_nt(gbv, gw_v[rows, :]) + dot_nt(ubv, uw_v[rows, :])

    first, second = 1 - yh, yh
    derive(xx(2))
    far_s[0] = block(xx(2), 0).astype(BF).reshape(2, 128, 256)
    send("fp0", far_s.at[0, first], far_r.at[0, first], xp)
    far_s[1] = block(xx(2), 1).astype(BF).reshape(2, 128, 256)
    send("fm0", far_s.at[1, first], far_r.at[1, first], xm)
    derive(xx(1))
    near_s[0, 1] = block(xx(1), 1).astype(BF).reshape(2, 128, 256)
    send("np10", near_s.at[0, 1, first], near_r.at[0, 1, first], xp)
    send("fp1", far_s.at[0, second], far_r.at[0, second], xp)
    derive(xx(-1))
    near_s[1, 0] = block(xx(-1), 0).astype(BF).reshape(2, 128, 256)
    send("nm00", near_s.at[1, 0, first], near_r.at[1, 0, first], xm)
    send("fm1", far_s.at[1, second], far_r.at[1, second], xm)
    near_f[0] = block(xx(1), 0).reshape(2, 128, 256)
    got("fp0")
    near_s[0, 0, first] = (near_f[0, first] + far_r[0, first].astype(F32)).astype(BF)
    send("np00", near_s.at[0, 0, first], near_r.at[0, 0, first], xp)
    send("np11", near_s.at[0, 1, second], near_r.at[0, 1, second], xp)
    near_f[1] = block(xx(-1), 1).reshape(2, 128, 256)
    got("fm0")
    near_s[1, 1, first] = (near_f[1, first] + far_r[1, first].astype(F32)).astype(BF)
    send("nm10", near_s.at[1, 1, first], near_r.at[1, 1, first], xm)
    send("nm01", near_s.at[1, 0, second], near_r.at[1, 0, second], xm)
    got("fp1")
    near_s[0, 0, second] = (near_f[0, second] + far_r[0, second].astype(F32)).astype(BF)
    send("np01", near_s.at[0, 0, second], near_r.at[0, 0, second], xp)
    got("fm1")
    near_s[1, 1, second] = (near_f[1, second] + far_r[1, second].astype(F32)).astype(BF)
    send("nm11", near_s.at[1, 1, second], near_r.at[1, 1, second], xm)
    derive(x)
    for side in range(2):
        own_f[side] = block(x, side).reshape(2, 128, 256)

    def total(side, e, part_of):
        got("np%d%d" % (side, part_of), "nm%d%d" % (side, part_of))
        near = near_r[0, side, e].astype(F32) + near_r[1, side, e].astype(F32)
        return own_f[side, e] + near

    for side in range(2):
        ys[side] = total(side, first, 0).astype(BF)
        send("yh%d" % side, ys.at[side], yr.at[side], yhp)

    def weight(dst, src):
        def step(n, carry):
            cols = pl.ds(pl.multiple_of(n * 256, 256), 256)
            right = src[:, :, cols].reshape(1024, 256)
            dst[:, cols] = dot_tn(acts_all[...].reshape(1024, 512), right).astype(BF)
            return carry

        lax.fori_loop(0, 4, step, 0)

    weight(o_gate, gb)
    weight(o_up, ub)
    for side in range(2):
        val = total(side, second, 1)
        got("yh%d" % side)
        o_in[:, 256 * side : 256 * side + 256] = (val + yr[side].astype(F32)).astype(BF)
    for i, units in enumerate(sent):
        behind = hid.at[0 : 16 * units]
        pltpu.make_async_copy(behind, behind, send_sem.at[i]).wait()


def leave(*refs):
    sems = refs[-1]
    copies = [pltpu.make_async_copy(refs[i], refs[4 + i], sems.at[i]) for i in range(4)]
    for copy in copies:
        copy.start()
    for copy in copies:
        copy.wait()


def per_device(activations, out_grad, gate_pre, up_pre, gate_weight, up_weight, down_weight):
    hbm = pl.BlockSpec(memory_space=pl.ANY)
    outs = pl.pallas_call(
        kernel,
        out_shape=(
            pltpu.VMEM((128, 512), BF),
            pltpu.VMEM((512, 1024), BF),
            pltpu.VMEM((512, 1024), BF),
            pltpu.VMEM((1024, 512), BF),
        ),
        in_specs=[hbm] * 7,
        out_specs=(pl.BlockSpec(memory_space=pltpu.VMEM),) * 4,
        scratch_shapes=[
            pltpu.VMEM((8, 128, 512), BF),
            pltpu.VMEM((8, 128, 512), BF),
            pltpu.VMEM((8, 2, 2, 32, 1024), BF),
            pltpu.VMEM((8, 2, 2, 32, 1024), BF),
            pltpu.VMEM((8, 2, 2, 32, 1024), BF),
            pltpu.VMEM((512, 1024), BF),
            pltpu.VMEM((512, 1024), BF),
            pltpu.VMEM((1024, 512), BF),
            pltpu.VMEM((8, 2, 2, 32, 1024), F32),
            pltpu.VMEM((8, 2, 32, 1024), F32),
            pltpu.VMEM((8, 32, 1024), BF),
            pltpu.VMEM((8, 32, 1024), BF),
            pltpu.VMEM((2, 32, W), BF),
            pltpu.VMEM((2, 32, W), BF),
            pltpu.VMEM((3, 2, 32, 1024), BF),
            pltpu.VMEM((3, 2, 32, 1024), BF),
            pltpu.VMEM((8, 128, 1024), F32),
            pltpu.VMEM((8, 128, 1024), F32),
            pltpu.VMEM((1024, 1024), BF),
            pltpu.VMEM((8, 128, 1024), BF),
            pltpu.VMEM((8, 128, 1024), BF),
            pltpu.VMEM((2, 2, 128, 256), BF),
            pltpu.VMEM((2, 2, 128, 256), BF),
            pltpu.VMEM((2, 2, 2, 128, 256), BF),
            pltpu.VMEM((2, 2, 2, 128, 256), BF),
            pltpu.VMEM((2, 2, 128, 256), F32),
            pltpu.VMEM((2, 2, 128, 256), F32),
            pltpu.VMEM((2, 128, 256), BF),
            pltpu.VMEM((2, 128, 256), BF),
            pltpu.SemaphoreType.DMA((N_SEND,)),
            pltpu.SemaphoreType.DMA((N_RECV,)),
            pltpu.SemaphoreType.DMA((7,)),
        ],
        compiler_params=pltpu.CompilerParams(
            collective_id=0, has_side_effects=True, vmem_limit_bytes=56 * 1024 * 1024
        ),
    )(activations, out_grad, gate_pre, up_pre, gate_weight, up_weight, down_weight)
    return pl.pallas_call(
        leave,
        out_shape=tuple(jax.ShapeDtypeStruct(o.shape, BF) for o in outs),
        in_specs=[hbm] * 4,
        out_specs=(hbm,) * 4,
        scratch_shapes=[pltpu.SemaphoreType.DMA((4,))],
        compiler_params=pltpu.CompilerParams(vmem_limit_bytes=1024 * 1024),
    )(*outs)


def solution(mesh):
    placed = (
        P("col", "row"),
        P("col", "row"),
        P("row", "col"),
        P("row", "col"),
        P("row", "col"),
        P("row", "col"),
        P("col", "row"),
    )
    return jax.shard_map(
        per_device,
        mesh=mesh,
        in_specs=placed,
        out_specs=(P("col", "row"), P("row", "col"), P("row", "col"), P("col", "row")),
        check_vma=False,
    )
```
